32 devices in a mesh: dp: 8 (over z, y), tensor: 4 (over x, core).
Axes of the slice: x: 2, y: 2, z: 4, core: 2. Of those that a mesh axis runs over, the one named last changes fastest.
Arguments:
- tokens: bfloat16 [3072, 1024], P(('dp', 'tensor')), may hold values from -6 to 6
- seq_lengths: int32 [8, 8], P('dp'), may hold values from 1 to 192, 384 in all within a row
- ln1_gain: float32 [1024], replicated, may hold values from 0.5 to 1.5
- ln1_bias: float32 [1024], replicated, may hold values from -3 to 3
- ln2_gain: float32 [1024], replicated, may hold values from 0.5 to 1.5
- ln2_bias: float32 [1024], replicated, may hold values from -3 to 3
- qkv_weight: bfloat16 [1024, 3072], P(None, 'tensor'), as said below
- qkv_bias: float32 [3072], P('tensor'), may hold values from -3 to 3
- out_weight: bfloat16 [1024, 1024], P('tensor'), may hold values from -0.75 to 0.75
- out_bias: float32 [1024], replicated, may hold values from -3 to 3
- up_weight: bfloat16 [1024, 4096], P(None, 'tensor'), may hold values from -0.1875 to 0.1875
- up_bias: float32 [4096], P('tensor'), may hold values from -3 to 3
- down_weight: bfloat16 [4096, 1024], P('tensor'), may hold values from -0.125 to 0.125
- down_bias: float32 [1024], replicated, may hold values from -3 to 3
- cotangent: bfloat16 [3072, 1024], P(('dp', 'tensor')), may hold values from -6 to 6
Outputs:
- output: bfloat16 [3072, 1024], P(('dp', 'tensor'))
- grad_input: bfloat16 [3072, 1024], P(('dp', 'tensor'))
- grad_ln1_gain: float32 [1024], replicated
- grad_ln1_bias: float32 [1024], replicated
- grad_ln2_gain: float32 [1024], replicated
- grad_ln2_bias: float32 [1024], replicated
- grad_qkv_weight: float32 [1024, 3072], P('dp', 'tensor')
- grad_qkv_bias: float32 [3072], P('tensor')
- grad_out_weight: float32 [1024, 1024], P('tensor', 'dp')
- grad_out_bias: float32 [1024], replicated
- grad_up_weight: float32 [1024, 4096], P('dp', 'tensor')
- grad_up_bias: float32 [4096], P('tensor')
- grad_down_weight: float32 [4096, 1024], P('tensor', 'dp')
- grad_down_bias: float32 [1024], replicated
The draws below stay inside these ranges and needn't reach their ends.
Inputs may be any that keep to these rules, and one draw needn't show every extreme that they name: `seq_lengths`: each row sums to 384, and its longest sequence is exactly 192. `qkv_weight`: A joined projection of fan-in 1024; columns of head h at h * 3 * 64 for queries, keys, then values.
All inputs are finite; a program needn't handle non-finite values.
Results may differ from the reference program's by a relative error of at most 0.0096.
Values may be sent and summed in bfloat16 or wider, within the bound.
No kernel may reach another device: no remote copies, remote signals or barrier semaphores. Data moves between devices by JAX's collectives and lax.ppermute only.
A program may use at most 128 MiB of HBM per device.

```python
import math
import jax
import jax.numpy as jnp
import numpy as np
from jax import lax

D = 1024
HEADS = 16
HD = 64
ROT = 16
FF = 4096
GROUP_TOK = 384
SEQS = 8
MAXLEN = 192
TOKENS = 3072
N_DP = 8


def draw_qkv_weight(key, part):
    first_key = jax.random.fold_in(key, 0)
    base = jax.random.normal(first_key, (D, HEADS, 3, HD), jnp.float32) * D ** (-0.5)
    return base.reshape(D, 3 * D).astype(jnp.bfloat16)


def spiked(drawn, stream_key, source, target, blocks, factor):
    owner, partner = [(jnp.arange(drawn.shape[axis_at]) // (drawn.shape[axis_at] // blocks)).reshape([-1 if axis == axis_at else 1 for axis in range(drawn.ndim)]) for axis_at in (source, target)]
    chosen = jax.random.permutation(stream_key, blocks)[partner]
    strong = (owner == chosen) | (owner == (partner + blocks // 2) % blocks)
    return jnp.where(strong, factor * drawn, drawn)


def steps_of(own_key, shape, shards, smallest, largest):
    def one(dim, shards_of):
        steps = jax.random.uniform(jax.random.fold_in(jax.random.fold_in(own_key, 6), dim), (shards_of,), jnp.float32, smallest / len(shards), largest / len(shards))
        return jnp.repeat(jnp.exp(steps), shape[dim] // shards_of).reshape((-1,) + (1,) * (len(shape) - dim - 1))

    factor_of = one(*shards[0])
    for cut in shards[1:]:
        factor_of = factor_of * one(*cut)
    return factor_of


def profile(amount, total, reach, slope):
    portions = [(1 << 20) // math.isqrt(rank ** slope) + 1 for rank in range(2, amount + 1)]
    surplus, given = total - reach - (amount - 1), [1] * (amount - 1)
    while surplus > 0:
        movable = [i for i in range(amount - 1) if given[i] < reach]
        whole, remaining = sum([portions[i] for i in movable]), surplus
        for i in movable:
            extra = min(reach - given[i], max(1, remaining * portions[i] // whole), surplus)
            given[i] = given[i] + extra
            surplus = surplus - extra
    return np.array([reach] + given)


def uneven(own_key, number_of, total, limit, skew):
    if number_of == 2:
        one = jax.random.randint(own_key, (), max(1, total - limit), min(limit, total - 1) + 1)
        return jnp.stack([one, total - one])
    tallies = jnp.asarray(profile(number_of, total, limit, skew), jnp.int32)
    couples = (number_of - 1) // 2
    giver, sink = tallies[1:1 + 2 * couples:2], tallies[2:2 + 2 * couples:2]
    room = jnp.minimum(giver - 1, limit - sink)
    moved = jax.random.randint(jax.random.fold_in(own_key, 1), (couples,), 0, 1 << 20) % (room + 1)
    tallies = tallies.at[1:1 + 2 * couples:2].set(giver - moved).at[2:2 + 2 * couples:2].set(sink + moved)
    return tallies[jax.random.permutation(jax.random.fold_in(own_key, 2), number_of)]


def normal_values(own_key, dims, scale, bound, pieces=(), held_as=jnp.bfloat16):
    result = scale * jax.random.normal(own_key, dims, jnp.float32)
    if pieces:
        result = result * steps_of(own_key, dims, pieces, -0.22, 0.18)
    return jnp.clip(result, -bound, bound).astype(held_as)


def noise_with(own_key, dims, spread, limit, shards, heavy, kind=jnp.bfloat16):
    values = spread * jax.random.normal(own_key, dims, jnp.float32)
    if shards:
        values = values * steps_of(own_key, dims, shards, -0.22, 0.18)
    return jnp.clip(spiked(values, jax.random.fold_in(own_key, 3), *heavy), -limit, limit).astype(kind)


def setup_inputs(seed: int = 0) -> dict:
    splits = jax.random.split(jax.random.key(seed), 16)
    tokens = noise_with(splits[0], (TOKENS, D), 1.0, 6.0, ((0, 32),), (0, 1, 32, 2.75))
    seq_lengths = jax.vmap(lambda own: uneven(own, SEQS, GROUP_TOK, MAXLEN, 2))(jax.random.split(splits[1], N_DP)).reshape((N_DP, SEQS)).astype(jnp.int32)
    ln1_gain = jnp.clip(1.0 + 0.1 * jax.random.normal(splits[2], (D,), jnp.float32), 0.5, 1.5)
    ln1_bias = normal_values(splits[3], (D,), 0.3, 3.0, (), jnp.float32)
    ln2_gain = jnp.clip(1.0 + 0.1 * jax.random.normal(splits[4], (D,), jnp.float32), 0.5, 1.5)
    ln2_bias = normal_values(splits[5], (D,), 0.3, 3.0, (), jnp.float32)
    qkv_weight = draw_qkv_weight(jax.random.fold_in(splits[15], 71), 0)
    qkv_bias = normal_values(splits[7], (3 * D,), 0.5, 3.0, ((0, 4),), jnp.float32)
    out_weight = normal_values(splits[8], (D, D), (D // 16) ** -0.5, 0.75, ((0, 4),))
    out_bias = normal_values(splits[9], (D,), 0.5, 3.0, (), jnp.float32)
    up_weight = normal_values(splits[10], (D, FF), D ** -0.5, 0.1875, ((1, 4),))
    up_bias = normal_values(splits[11], (FF,), 0.5, 3.0, ((0, 4),), jnp.float32)
    down_weight = normal_values(splits[12], (FF, D), (FF // 2) ** -0.5, 0.125, ((0, 4),))
    down_bias = normal_values(splits[13], (D,), 0.5, 3.0, (), jnp.float32)
    cotangent = noise_with(splits[14], (TOKENS, D), 1.0, 6.0, ((0, 32),), (0, 1, 32, 2.75))
    return {"tokens": tokens, "seq_lengths": seq_lengths, "ln1_gain": ln1_gain, "ln1_bias": ln1_bias, "ln2_gain": ln2_gain, "ln2_bias": ln2_bias, "qkv_weight": qkv_weight, "qkv_bias": qkv_bias, "out_weight": out_weight, "out_bias": out_bias, "up_weight": up_weight, "up_bias": up_bias, "down_weight": down_weight, "down_bias": down_bias, "cotangent": cotangent}


epsilon = 1e-05
masked_score = 1e+30
inv_sqrt_two = 0.7071067811865476
inv_sqrt_two_pi = 0.3989422804014327

def sequence_layout(lengths_row, length_total):
    ends = jnp.cumsum(lengths_row).astype(jnp.int32)
    starts = ends - lengths_row
    token_ids = jnp.arange(length_total, dtype=jnp.int32)
    segment = lax.optimization_barrier(jnp.sum((token_ids[:, None] >= ends[None, :]).astype(jnp.int32), axis=1))
    member = segment[:, None] == jnp.arange(lengths_row.shape[0], dtype=jnp.int32)[None, :]
    first_token = lax.optimization_barrier(jnp.sum(jnp.where(member, starts[None, :], 0), axis=1)).astype(jnp.int32)
    return (segment, token_ids - first_token)

def rotary_tables(position, rot_dims):
    half_dims = rot_dims // 2
    freqs = 10000.0 ** (-(jnp.arange(half_dims, dtype=jnp.float32) * 2.0 / rot_dims))
    angles = position.astype(jnp.float32)[:, None] * freqs[None, :]
    return (jnp.cos(angles)[:, None, :], jnp.sin(angles)[:, None, :])

def rotate(values, cosine, sine, rot_dims):
    half_dims = rot_dims // 2
    first_half = values[..., :half_dims]
    second_half = values[..., half_dims:rot_dims]
    return jnp.concatenate([first_half * cosine - second_half * sine, second_half * cosine + first_half * sine, values[..., rot_dims:]], axis=-1)

def gelu_exact(inputs):
    return 0.5 * inputs * (1.0 + lax.erf(inputs * inv_sqrt_two))

def gelu_slope(inputs):
    return 0.5 * (1.0 + lax.erf(inputs * inv_sqrt_two)) + inputs * jnp.exp(-0.5 * inputs * inputs) * inv_sqrt_two_pi

def normalize(inputs):
    centered = inputs - lax.optimization_barrier(jnp.mean(inputs, axis=-1, keepdims=True))
    inv_std = lax.rsqrt(lax.optimization_barrier(jnp.mean(centered * centered, axis=-1, keepdims=True)) + epsilon)
    return (centered * inv_std, inv_std)

def reference(tokens, seq_lengths, ln1_gain, ln1_bias, ln2_gain, ln2_bias, qkv_weight, qkv_bias, out_weight, out_bias, up_weight, up_bias, down_weight, down_bias, cotangent):
    groups = seq_lengths.shape[0]
    length_total = tokens.shape[0] // groups
    width = tokens.shape[1]
    score_scale = 1.0 / math.sqrt(HD)
    token_ids = jnp.arange(length_total, dtype=jnp.int32)
    input_groups = tokens.reshape(groups, length_total, width)
    grad_groups = cotangent.reshape(groups, length_total, width)

    def group_step(totals, inputs_now):
        rows_in, rows_grad, lengths_row = inputs_now
        segment, position = sequence_layout(lengths_row, length_total)
        cosine, sine = rotary_tables(position, ROT)
        allowed = (segment[:, None] == segment[None, :]) & (token_ids[:, None] >= token_ids[None, :])
        rows_float = rows_in.astype(jnp.float32)
        normed, inv_std = normalize(rows_float)
        first_in = (normed * ln1_gain + ln1_bias).astype(jnp.bfloat16)
        second_in = (normed * ln2_gain + ln2_bias).astype(jnp.bfloat16)
        joined = (jnp.dot(first_in, qkv_weight, preferred_element_type=jnp.float32) + qkv_bias).reshape(length_total, HEADS, 3, HD)
        query = rotate(joined[:, :, 0], cosine, sine, ROT).astype(jnp.bfloat16).astype(jnp.float32)
        key_rows = rotate(joined[:, :, 1], cosine, sine, ROT).astype(jnp.bfloat16).astype(jnp.float32)
        value = joined[:, :, 2].astype(jnp.bfloat16).astype(jnp.float32)
        scores = jnp.einsum('qhd,khd->hqk', query, key_rows) * score_scale
        scores = jnp.where(allowed[None], scores, -masked_score)
        peak = lax.optimization_barrier(jnp.max(scores, axis=-1, keepdims=True))
        expo = jnp.exp(scores - peak)
        total = lax.optimization_barrier(jnp.sum(expo, axis=-1, keepdims=True))
        lse = peak + jnp.log(total)
        probs = (expo / total).astype(jnp.bfloat16).astype(jnp.float32)
        attended = jnp.einsum('hqk,khd->qhd', probs, value).astype(jnp.bfloat16)
        flat = attended.reshape(length_total, width)
        hidden = jnp.dot(second_in, up_weight, preferred_element_type=jnp.float32) + up_bias
        active = gelu_exact(hidden).astype(jnp.bfloat16)
        branch = jnp.dot(flat, out_weight, preferred_element_type=jnp.float32) + jnp.dot(active, down_weight, preferred_element_type=jnp.float32)
        output = (rows_float + branch + out_bias + down_bias).astype(jnp.bfloat16)
        grad_float = rows_grad.astype(jnp.float32)
        g_down = jnp.dot(active.T, rows_grad, preferred_element_type=jnp.float32)
        d_hidden = jnp.dot(rows_grad, down_weight.T, preferred_element_type=jnp.float32) * gelu_slope(hidden)
        g_up_bias = lax.optimization_barrier(jnp.sum(d_hidden, axis=0))
        d_hidden_b = d_hidden.astype(jnp.bfloat16)
        g_up = jnp.dot(second_in.T, d_hidden_b, preferred_element_type=jnp.float32)
        d_second = jnp.dot(d_hidden_b, up_weight.T, preferred_element_type=jnp.float32)
        g_out = jnp.dot(flat.T, rows_grad, preferred_element_type=jnp.float32)
        d_attended = jnp.dot(rows_grad, out_weight.T, preferred_element_type=jnp.float32).astype(jnp.bfloat16).astype(jnp.float32).reshape(length_total, HEADS, HD)
        probs_again = jnp.where(allowed[None], jnp.exp(scores - lse), 0.0)
        probs_again_b = probs_again.astype(jnp.bfloat16).astype(jnp.float32)
        d_value = jnp.einsum('hqk,qhd->khd', probs_again_b, d_attended)
        d_probs = jnp.einsum('qhd,khd->hqk', d_attended, value)
        delta = lax.optimization_barrier(jnp.sum(d_attended * attended.astype(jnp.float32), axis=-1)).T
        d_scores = (probs_again * (d_probs - delta[:, :, None]) * score_scale).astype(jnp.bfloat16).astype(jnp.float32)
        d_query = rotate(jnp.einsum('hqk,khd->qhd', d_scores, key_rows), cosine, -sine, ROT)
        d_key = rotate(jnp.einsum('hqk,qhd->khd', d_scores, query), cosine, -sine, ROT)
        d_joined = jnp.stack([d_query, d_key, d_value], axis=2).reshape(length_total, 3 * width)
        g_qkv_bias = lax.optimization_barrier(jnp.sum(d_joined, axis=0))
        d_joined_b = d_joined.astype(jnp.bfloat16)
        g_qkv = jnp.dot(first_in.T, d_joined_b, preferred_element_type=jnp.float32)
        d_first = jnp.dot(d_joined_b, qkv_weight.T, preferred_element_type=jnp.float32)
        mixed = d_first * ln1_gain + d_second * ln2_gain
        grad_in = inv_std * (mixed - lax.optimization_barrier(jnp.mean(mixed, axis=-1, keepdims=True)) - normed * lax.optimization_barrier(jnp.mean(mixed * normed, axis=-1, keepdims=True))) + grad_float
        grad_in = grad_in.astype(jnp.bfloat16)
        updates = (lax.optimization_barrier(jnp.sum(d_first * normed, axis=0)), lax.optimization_barrier(jnp.sum(d_first, axis=0)), lax.optimization_barrier(jnp.sum(d_second * normed, axis=0)), lax.optimization_barrier(jnp.sum(d_second, axis=0)), g_qkv, g_qkv_bias, g_out, lax.optimization_barrier(jnp.sum(grad_float, axis=0)), g_up, g_up_bias, g_down)
        new_totals = tuple((old + new for old, new in zip(totals, updates)))
        return (new_totals, (output, grad_in))
    zero_vec = jnp.zeros((width,), jnp.float32)
    start_totals = (zero_vec, zero_vec, zero_vec, zero_vec, jnp.zeros(qkv_weight.shape, jnp.float32), jnp.zeros(qkv_bias.shape, jnp.float32), jnp.zeros(out_weight.shape, jnp.float32), zero_vec, jnp.zeros(up_weight.shape, jnp.float32), jnp.zeros(up_bias.shape, jnp.float32), jnp.zeros(down_weight.shape, jnp.float32))
    totals, stacked = lax.scan(group_step, start_totals, (input_groups, grad_groups, seq_lengths))
    output = stacked[0].reshape(tokens.shape)
    grad_input = stacked[1].reshape(tokens.shape)
    return (output, grad_input, totals[0], totals[1], totals[2], totals[3], totals[4], totals[5], totals[6], totals[7], totals[8], totals[9], totals[10], totals[7])
```

```python
import math

import jax
import jax.numpy as jnp
from jax import lax
from jax.sharding import PartitionSpec as P

HD = 64
ROT = 16


epsilon = 1e-05
masked_score = 1e30
inv_sqrt_two = 0.7071067811865476
inv_sqrt_two_pi = 0.3989422804014327


def sequence_layout(lengths_row, length_total):
    ends = jnp.cumsum(lengths_row)
    starts = ends - lengths_row
    token_ids = jnp.arange(length_total, dtype=jnp.int32)
    segment = jnp.sum((token_ids[:, None] >= ends[None, :]).astype(jnp.int32), axis=1)
    member = segment[:, None] == jnp.arange(lengths_row.shape[0], dtype=jnp.int32)[None, :]
    first_token = jnp.sum(jnp.where(member, starts[None, :], 0), axis=1)
    return (segment, token_ids - first_token)


def rotary_tables(position, rot_dims):
    half_dims = rot_dims // 2
    freqs = 10000.0 ** (-(jnp.arange(half_dims, dtype=jnp.float32) * 2.0 / rot_dims))
    angles = position.astype(jnp.float32)[:, None] * freqs[None, :]
    return (jnp.cos(angles)[:, None, :], jnp.sin(angles)[:, None, :])


def rotate(values, cosine, sine, rot_dims):
    half_dims = rot_dims // 2
    first_half = values[..., :half_dims]
    second_half = values[..., half_dims:rot_dims]
    return jnp.concatenate(
        [
            first_half * cosine - second_half * sine,
            second_half * cosine + first_half * sine,
            values[..., rot_dims:],
        ],
        axis=-1,
    )


def normalize(inputs):
    centered = inputs - jnp.mean(inputs, axis=-1, keepdims=True)
    inv_std = lax.rsqrt(jnp.mean(centered * centered, axis=-1, keepdims=True) + epsilon)
    return (centered * inv_std, inv_std)


def swap(array, axis, bit):
    count = lax.axis_size(axis)
    return lax.ppermute(array, axis, [(i, i ^ (1 << bit)) for i in range(count)])


def axis_bits(axis):
    return lax.axis_size(axis).bit_length() - 1


def relative_blocks(array, axis, bits, dim):
    count = lax.axis_size(axis)
    own = lax.axis_index(axis)
    size = array.shape[dim] // count
    pieces = []
    for place in range(count):
        relative = 0
        for depth, bit in enumerate(bits):
            if (place >> (len(bits) - 1 - depth)) & 1:
                relative |= 1 << bit
        pieces.append(lax.dynamic_slice_in_dim(array, (own ^ relative) * size, size, dim))
    return jnp.concatenate(pieces, axis=dim)


def halves(array, dim):
    middle = array.shape[dim] // 2
    return (
        lax.slice_in_dim(array, 0, middle, axis=dim),
        lax.slice_in_dim(array, middle, 2 * middle, axis=dim),
    )


def fold(keep, send, axis, bits, dim):
    for depth, bit in enumerate(bits):
        arrived = swap(send, axis, bit)
        total = keep + arrived.astype(jnp.float32)
        if depth + 1 < len(bits):
            keep, send = halves(total, dim)
            send = send.astype(jnp.bfloat16)
    return total


def all_sum(array, axis, bits):
    for bit in bits:
        array = array + swap(array, axis, bit)
    return array


def dot(left, right, dims):
    return lax.dot_general(left, right, (dims, ((), ())), preferred_element_type=jnp.float32)


TN = ((0,), (0,))
NN = ((1,), (0,))
NT = ((1,), (1,))


def shards(
    tokens,
    seq_lengths,
    ln1_gain,
    ln1_bias,
    ln2_gain,
    ln2_bias,
    qkv_weight,
    qkv_bias,
    out_weight,
    out_bias,
    up_weight,
    up_bias,
    down_weight,
    down_bias,
    cotangent,
):
    row_count = tokens.shape[0]
    width = tokens.shape[1]
    tensor_bits = list(range(axis_bits("tensor")))
    dp_bits = list(range(axis_bits("dp")))
    y_first = dp_bits
    z_first = dp_bits[1:2] + dp_bits[0:1] + dp_bits[2:]
    length_total = row_count * lax.axis_size("tensor")
    local_heads = qkv_weight.shape[1] // (3 * HD)
    score_scale = 1.0 / math.sqrt(HD)
    token_ids = jnp.arange(length_total, dtype=jnp.int32)
    segment, position = sequence_layout(seq_lengths[0], length_total)
    cosine, sine = rotary_tables(position, ROT)

    def gather(rows):
        own = lax.axis_index("tensor")
        for bit in reversed(tensor_bits):
            other = swap(rows, "tensor", bit)
            high = ((own >> bit) & 1) == 1
            rows = jnp.concatenate(
                [jnp.where(high, other, rows), jnp.where(high, rows, other)], axis=0
            )
        count = lax.axis_size("tensor")
        blocks = [lax.slice_in_dim(rows, i * row_count, (i + 1) * row_count) for i in range(count)]
        order = []
        for index in range(count):
            place = 0
            for bit in tensor_bits:
                if (index >> bit) & 1:
                    place |= 1 << (len(tensor_bits) - 1 - bit)
            order.append(blocks[place])
        return jnp.concatenate(order, axis=0)

    whole_rows = gather(tokens)
    grad_rows_all = gather(cotangent)
    whole_normed = normalize(whole_rows.astype(jnp.float32))[0]
    first_in = (whole_normed * ln1_gain + ln1_bias).astype(jnp.bfloat16)
    second_in = (whole_normed * ln2_gain + ln2_bias).astype(jnp.bfloat16)

    first_rel = halves(relative_blocks(first_in, "dp", z_first, 1), 1)
    second_rel = halves(relative_blocks(second_in, "dp", y_first, 1), 1)
    grad_rel = halves(relative_blocks(grad_rows_all, "dp", y_first, 1), 1)

    hidden = dot(second_in, up_weight, NN) + up_bias
    cumulative = 0.5 * (1.0 + lax.erf(hidden * inv_sqrt_two))
    active = (hidden * cumulative).astype(jnp.bfloat16)
    slope = cumulative + hidden * jnp.exp(-0.5 * hidden * hidden) * inv_sqrt_two_pi
    down_send = dot(active, grad_rel[1], TN).astype(jnp.bfloat16)
    down_keep = dot(active, grad_rel[0], TN)
    grad_down_weight = fold(down_keep, down_send, "dp", y_first, 1)

    d_hidden = dot(grad_rows_all, down_weight, NT) * slope
    g_up_bias = jnp.sum(d_hidden, axis=0)
    d_hidden_b = d_hidden.astype(jnp.bfloat16)
    up_send = dot(second_rel[1], d_hidden_b, TN).astype(jnp.bfloat16)
    up_keep = dot(second_rel[0], d_hidden_b, TN)
    grad_up_weight = fold(up_keep, up_send, "dp", y_first, 0)

    joined = (dot(first_in, qkv_weight, NN) + qkv_bias).reshape(length_total, local_heads, 3, HD)
    query = rotate(joined[:, :, 0], cosine, sine, ROT).astype(jnp.bfloat16)
    key_rows = rotate(joined[:, :, 1], cosine, sine, ROT).astype(jnp.bfloat16)
    value = joined[:, :, 2].astype(jnp.bfloat16)
    allowed = (segment[:, None] == segment[None, :]) & (token_ids[:, None] >= token_ids[None, :])
    scores = (
        jnp.einsum("qhd,khd->hqk", query, key_rows, preferred_element_type=jnp.float32)
        * score_scale
    )
    scores = jnp.where(allowed[None], scores, -masked_score)
    peak = jnp.max(scores, axis=-1, keepdims=True)
    expo = jnp.exp(scores - peak)
    total = jnp.sum(expo, axis=-1, keepdims=True)
    probs_again = expo / total
    probs = probs_again.astype(jnp.bfloat16)
    attended = jnp.einsum("hqk,khd->qhd", probs, value, preferred_element_type=jnp.float32).astype(
        jnp.bfloat16
    )
    flat = attended.reshape(length_total, local_heads * HD)

    d_attended = (
        dot(grad_rows_all, out_weight, NT)
        .astype(jnp.bfloat16)
        .reshape(length_total, local_heads, HD)
    )
    d_value = jnp.einsum("hqk,qhd->khd", probs, d_attended, preferred_element_type=jnp.float32)
    d_probs = jnp.einsum("qhd,khd->hqk", d_attended, value, preferred_element_type=jnp.float32)
    delta = jnp.sum(d_attended.astype(jnp.float32) * attended.astype(jnp.float32), axis=-1).T
    d_scores = (probs_again * (d_probs - delta[:, :, None]) * score_scale).astype(jnp.bfloat16)
    d_query = jnp.einsum("hqk,khd->qhd", d_scores, key_rows, preferred_element_type=jnp.float32)
    d_key = jnp.einsum("hqk,qhd->khd", d_scores, query, preferred_element_type=jnp.float32)
    d_query = rotate(d_query, cosine, -sine, ROT)
    d_key = rotate(d_key, cosine, -sine, ROT)
    d_joined = jnp.stack([d_query, d_key, d_value], axis=2).reshape(
        length_total, 3 * local_heads * HD
    )
    g_qkv_bias = jnp.sum(d_joined, axis=0)
    d_joined_b = d_joined.astype(jnp.bfloat16)
    qkv_send = dot(first_rel[1], d_joined_b, TN).astype(jnp.bfloat16)
    qkv_keep = dot(first_rel[0], d_joined_b, TN)
    grad_qkv_weight = fold(qkv_keep, qkv_send, "dp", z_first, 0)

    out_send = dot(flat, grad_rel[1], TN).astype(jnp.bfloat16)
    out_keep = dot(flat, grad_rel[0], TN)
    grad_out_weight = fold(out_keep, out_send, "dp", y_first, 1)

    def token_sum(partial):
        ordered = relative_blocks(partial, "tensor", tensor_bits, 0)
        keep, send = halves(ordered, 0)
        return fold(keep, send.astype(jnp.bfloat16), "tensor", tensor_bits, 0)

    d_first = dot(d_joined_b, qkv_weight, NT)
    d_second = dot(d_hidden_b, up_weight, NT)
    mixed = token_sum(d_first * ln1_gain + d_second * ln2_gain)
    branch = token_sum(dot(flat, out_weight, NN) + dot(active, down_weight, NN))

    norm_sums = jnp.concatenate(
        [
            jnp.sum(d_first * whole_normed, axis=0),
            jnp.sum(d_first, axis=0),
            jnp.sum(d_second * whole_normed, axis=0),
            jnp.sum(d_second, axis=0),
        ]
    )
    norm_sums = all_sum(norm_sums, "tensor", tensor_bits)
    bias_total = jnp.sum(grad_rows_all.astype(jnp.float32), axis=0)
    sums = all_sum(
        jnp.concatenate([norm_sums, bias_total, g_up_bias, g_qkv_bias]), "dp", dp_bits
    )
    gain_one, shift_one, gain_two, shift_two, bias_total = (
        sums[i * width : (i + 1) * width] for i in range(5)
    )
    rest = sums[5 * width :]
    grad_up_bias = rest[: g_up_bias.shape[0]]
    grad_qkv_bias = rest[g_up_bias.shape[0] :]

    rows_float = tokens.astype(jnp.float32)
    normed, inv_std = normalize(rows_float)
    output = (rows_float + branch + out_bias + down_bias).astype(jnp.bfloat16)
    grad_float = cotangent.astype(jnp.float32)
    grad_input = (
        inv_std
        * (
            mixed
            - jnp.mean(mixed, axis=-1, keepdims=True)
            - normed * jnp.mean(mixed * normed, axis=-1, keepdims=True)
        )
        + grad_float
    )
    grad_input = grad_input.astype(jnp.bfloat16)
    return (
        output,
        grad_input,
        gain_one,
        shift_one,
        gain_two,
        shift_two,
        grad_qkv_weight,
        grad_qkv_bias,
        grad_out_weight,
        bias_total,
        grad_up_weight,
        grad_up_bias,
        grad_down_weight,
        bias_total,
    )


def solution(mesh):
    placed = (
        P(("dp", "tensor"), None),
        P("dp", None),
        P(),
        P(),
        P(),
        P(),
        P(None, "tensor"),
        P("tensor"),
        P("tensor", None),
        P(),
        P(None, "tensor"),
        P("tensor"),
        P("tensor", None),
        P(),
        P(("dp", "tensor"), None),
    )
    return jax.shard_map(
        shards,
        mesh=mesh,
        in_specs=placed,
        out_specs=(
            P(("dp", "tensor"), None),
            P(("dp", "tensor"), None),
            P(),
            P(),
            P(),
            P(),
            P("dp", "tensor"),
            P("tensor"),
            P("tensor", "dp"),
            P(),
            P("dp", "tensor"),
            P("tensor"),
            P("tensor", "dp"),
            P(),
        ),
        check_vma=False,
    )
```

```python
import math

import jax
import jax.numpy as jnp
from jax import lax
from jax.experimental import pallas as pl
from jax.experimental.pallas import tpu as pltpu
from jax.sharding import PartitionSpec as P


HD = 64
ROT = 16


epsilon = 1e-05
masked_score = 1e30
inv_sqrt_two = 0.7071067811865476
inv_sqrt_two_pi = 0.3989422804014327


TN = ((0,), (0,))
NN = ((1,), (0,))
NT = ((1,), (1,))


def sequence_layout(lengths_row, token_ids):
    ends = jnp.cumsum(lengths_row)
    starts = ends - lengths_row
    segment = jnp.sum((token_ids[:, None] >= ends[None, :]).astype(jnp.int32), axis=1)
    member = segment[:, None] == jnp.arange(lengths_row.shape[0], dtype=jnp.int32)[None, :]
    first_token = jnp.sum(jnp.where(member, starts[None, :], 0), axis=1)
    return first_token


def rotary_tables(position, rot_dims):
    half_dims = rot_dims // 2
    freqs = 10000.0 ** (-(jnp.arange(half_dims, dtype=jnp.float32) * 2.0 / rot_dims))
    angles = position.astype(jnp.float32)[:, None] * freqs[None, :]
    cosine = jnp.cos(angles)
    sine = jnp.sin(angles)
    rows = position.shape[0]
    none = jnp.zeros_like(sine)
    ones = jnp.ones((rows, HD - rot_dims), jnp.float32)
    zeros = jnp.zeros((rows, HD - rot_dims), jnp.float32)
    direct = [cosine, cosine, ones]
    later = [-sine, none, zeros]
    earlier = [none, sine, zeros]
    one_head = jnp.ones((rows, HD), jnp.float32)
    no_head = jnp.zeros((rows, HD), jnp.float32)
    return tuple(
        jnp.concatenate(part + part + [last], axis=1)
        for part, last in ((direct, one_head), (later, no_head), (earlier, no_head))
    )


def attention_body(
    first_ref,
    weight_ref,
    bias_ref,
    grad_ref,
    out_ref,
    direct_ref,
    later_ref,
    earlier_ref,
    starts_ref,
    ids_ref,
    keys_ref,
    flat_ref,
    d_joined_ref,
    bias_sum_ref,
    turned_ref,
    d_turned_ref,
):
    heads = weight_ref.shape[1] // (3 * HD)
    half = ROT // 2
    scale = 1.0 / math.sqrt(HD)

    def columns(head, kind):
        start = (3 * head + kind) * HD
        return slice(start, start + HD)

    joined = (
        lax.dot_general(
            first_ref[...], weight_ref[...], (NN, ((), ())), preferred_element_type=jnp.float32
        )
        + bias_ref[...]
    )
    total = joined.shape[1]

    def tiled(ref):
        return jnp.concatenate([ref[...]] * heads, axis=1)

    direct = tiled(direct_ref)
    later = tiled(later_ref)
    earlier = tiled(earlier_ref)
    turned_ref[...] = (
        joined * direct
        + pltpu.roll(joined, total - half, 1) * later
        + pltpu.roll(joined, half, 1) * earlier
    ).astype(jnp.bfloat16)
    d_attended_all = lax.dot_general(
        grad_ref[...], out_ref[...], (NT, ((), ())), preferred_element_type=jnp.float32
    ).astype(jnp.bfloat16)
    allowed = (keys_ref[...] >= starts_ref[...]) & (keys_ref[...] <= ids_ref[...])

    def product(left, right, dims):
        return lax.dot_general(left, right, (dims, ((), ())), preferred_element_type=jnp.float32)

    for head in range(heads):
        query = turned_ref[:, columns(head, 0)]
        key = turned_ref[:, columns(head, 1)]
        value = turned_ref[:, columns(head, 2)]
        d_attended = d_attended_all[:, head * HD : (head + 1) * HD]
        scores = jnp.where(allowed, product(query, key, NT) * scale, -masked_score)
        peak = jnp.max(scores, axis=1, keepdims=True)
        expo = jnp.exp(scores - peak)
        probs = expo / jnp.sum(expo, axis=1, keepdims=True)
        probs_b = probs.astype(jnp.bfloat16)
        attended = product(probs_b, value, NN).astype(jnp.bfloat16)
        flat_ref[:, head * HD : (head + 1) * HD] = attended
        d_probs = product(d_attended, value, NT)
        delta = jnp.sum(
            d_attended.astype(jnp.float32) * attended.astype(jnp.float32), axis=1, keepdims=True
        )
        d_scores = (probs * (d_probs - delta) * scale).astype(jnp.bfloat16)
        d_turned_ref[:, columns(head, 0)] = product(d_scores, key, NN)
        d_turned_ref[:, columns(head, 1)] = product(d_scores, query, TN)
        d_turned_ref[:, columns(head, 2)] = product(probs_b, d_attended, TN)
    d_turned = d_turned_ref[...]
    d_joined = (
        d_turned * direct
        - pltpu.roll(d_turned, total - half, 1) * later
        - pltpu.roll(d_turned, half, 1) * earlier
    )
    bias_sum_ref[...] = jnp.sum(d_joined, axis=0, keepdims=True)
    d_joined_ref[...] = d_joined.astype(jnp.bfloat16)


def attention(first_in, weight, bias, grad_rows, out_weight, tables, first_token, token_ids):
    rows = first_in.shape[0]
    columns = weight.shape[1]
    in_vmem = pl.BlockSpec(memory_space=pltpu.VMEM)
    return pl.pallas_call(
        attention_body,
        in_specs=[in_vmem] * 11,
        out_specs=[in_vmem] * 3,
        out_shape=[
            jax.ShapeDtypeStruct((rows, columns // 3), jnp.bfloat16),
            jax.ShapeDtypeStruct((rows, columns), jnp.bfloat16),
            jax.ShapeDtypeStruct((1, columns), jnp.float32),
        ],
        scratch_shapes=[
            pltpu.VMEM((rows, columns), jnp.bfloat16),
            pltpu.VMEM((rows, columns), jnp.float32),
        ],
        name="attention",
    )(
        first_in,
        weight,
        bias[None, :],
        grad_rows,
        out_weight,
        *tables,
        first_token[:, None],
        token_ids[:, None],
        token_ids[None, :],
    )


def normalize(inputs):
    centered = inputs - jnp.mean(inputs, axis=-1, keepdims=True)
    inv_std = lax.rsqrt(jnp.mean(centered * centered, axis=-1, keepdims=True) + epsilon)
    return (centered * inv_std, inv_std)


def swap(array, axis, bit):
    count = lax.axis_size(axis)
    return lax.ppermute(array, axis, [(i, i ^ (1 << bit)) for i in range(count)])


def axis_bits(axis):
    return lax.axis_size(axis).bit_length() - 1


def relatives(bits):
    found = [0]
    for bit in reversed(bits):
        found = found + [relative | (1 << bit) for relative in found]
    return found


def relative_blocks(array, axis, bits, dim):
    own = lax.axis_index(axis)
    size = array.shape[dim] // lax.axis_size(axis)
    pieces = [
        lax.dynamic_slice_in_dim(array, (own ^ relative) * size, size, dim)
        for relative in relatives(bits)
    ]
    return jnp.concatenate(pieces, axis=dim)


def halves(array, dim):
    middle = array.shape[dim] // 2
    return (
        lax.slice_in_dim(array, 0, middle, axis=dim),
        lax.slice_in_dim(array, middle, 2 * middle, axis=dim),
    )


def fold(keep, send, axis, bits, dim):
    for depth, bit in enumerate(bits):
        arrived = swap(send, axis, bit)
        total = keep + arrived.astype(jnp.float32)
        if depth + 1 < len(bits):
            keep, send = halves(total, dim)
            send = send.astype(jnp.bfloat16)
    return total


def all_sum(array, axis, bits):
    for bit in bits:
        array = array + swap(array, axis, bit)
    return array


def dot(left, right, dims):
    return lax.dot_general(left, right, (dims, ((), ())), preferred_element_type=jnp.float32)


def shards(
    tokens,
    seq_lengths,
    ln1_gain,
    ln1_bias,
    ln2_gain,
    ln2_bias,
    qkv_weight,
    qkv_bias,
    out_weight,
    out_bias,
    up_weight,
    up_bias,
    down_weight,
    down_bias,
    cotangent,
):
    row_count = tokens.shape[0]
    width = tokens.shape[1]
    tensor_bits = list(range(axis_bits("tensor")))
    dp_bits = list(range(axis_bits("dp")))
    y_first = dp_bits
    z_first = dp_bits[1:2] + dp_bits[0:1] + dp_bits[2:]
    own_rank = lax.axis_index("tensor")
    token_ids = jnp.concatenate(
        [
            (own_rank ^ relative) * row_count + jnp.arange(row_count, dtype=jnp.int32)
            for relative in relatives(tensor_bits)
        ]
    )
    first_token = sequence_layout(seq_lengths[0], token_ids)
    tables = rotary_tables(token_ids - first_token, ROT)

    def gather(rows):
        for bit in reversed(tensor_bits):
            rows = jnp.concatenate([rows, swap(rows, "tensor", bit)], axis=0)
        return rows

    whole_rows = gather(tokens)
    grad_rows_all = gather(cotangent)
    whole_normed = normalize(whole_rows.astype(jnp.float32))[0]
    first_in = (whole_normed * ln1_gain + ln1_bias).astype(jnp.bfloat16)
    second_in = (whole_normed * ln2_gain + ln2_bias).astype(jnp.bfloat16)

    first_rel = halves(relative_blocks(first_in, "dp", y_first, 1), 1)
    second_rel = halves(relative_blocks(second_in, "dp", z_first, 1), 1)
    grad_rel = halves(relative_blocks(grad_rows_all, "dp", y_first, 1), 1)

    hidden = dot(second_in, up_weight, NN) + up_bias
    cumulative = 0.5 * (1.0 + lax.erf(hidden * inv_sqrt_two))
    active = (hidden * cumulative).astype(jnp.bfloat16)
    slope = cumulative + hidden * jnp.exp(-0.5 * hidden * hidden) * inv_sqrt_two_pi
    down_send = dot(active, grad_rel[1], TN).astype(jnp.bfloat16)
    down_keep = dot(active, grad_rel[0], TN)
    grad_down_weight = fold(down_keep, down_send, "dp", y_first, 1)

    d_hidden = dot(grad_rows_all, down_weight, NT) * slope
    d_hidden_b = d_hidden.astype(jnp.bfloat16)
    g_up_bias = jnp.sum(d_hidden, axis=0)
    up_send = dot(second_rel[1], d_hidden_b, TN).astype(jnp.bfloat16)
    up_keep = dot(second_rel[0], d_hidden_b, TN)
    grad_up_weight = fold(up_keep, up_send, "dp", z_first, 0)

    flat, d_joined_b, g_qkv_bias = attention(
        first_in,
        qkv_weight,
        qkv_bias,
        grad_rows_all,
        out_weight,
        tables,
        first_token,
        token_ids,
    )
    g_qkv_bias = g_qkv_bias[0]
    qkv_send = dot(first_rel[1], d_joined_b, TN).astype(jnp.bfloat16)
    qkv_keep = dot(first_rel[0], d_joined_b, TN)
    grad_qkv_weight = fold(qkv_keep, qkv_send, "dp", y_first, 0)

    out_send = dot(flat, grad_rel[1], TN).astype(jnp.bfloat16)
    out_keep = dot(flat, grad_rel[0], TN)
    grad_out_weight = fold(out_keep, out_send, "dp", y_first, 1)

    def token_sum(partial):
        keep, send = halves(partial, 0)
        return fold(keep, send.astype(jnp.bfloat16), "tensor", tensor_bits, 0)

    d_first = dot(d_joined_b, qkv_weight, NT)
    d_second = dot(d_hidden_b, up_weight, NT)
    mixed = token_sum(d_first * ln1_gain + d_second * ln2_gain)
    branch = token_sum(dot(flat, out_weight, NN) + dot(active, down_weight, NN))

    norm_sums = jnp.concatenate(
        [
            jnp.sum(d_first * whole_normed, axis=0),
            jnp.sum(d_first, axis=0),
            jnp.sum(d_second * whole_normed, axis=0),
            jnp.sum(d_second, axis=0),
        ]
    )
    norm_sums = all_sum(norm_sums, "tensor", tensor_bits)
    bias_total = jnp.sum(grad_rows_all.astype(jnp.float32), axis=0)
    sums = all_sum(
        jnp.concatenate([norm_sums, bias_total, g_up_bias, g_qkv_bias]), "dp", dp_bits
    )
    gain_one, shift_one, gain_two, shift_two, bias_total = (
        sums[i * width : (i + 1) * width] for i in range(5)
    )
    rest = sums[5 * width :]
    grad_up_bias = rest[: g_up_bias.shape[0]]
    grad_qkv_bias = rest[g_up_bias.shape[0] :]

    rows_float = tokens.astype(jnp.float32)
    normed, inv_std = normalize(rows_float)
    output = (rows_float + branch + out_bias + down_bias).astype(jnp.bfloat16)
    grad_float = cotangent.astype(jnp.float32)
    grad_input = (
        inv_std
        * (
            mixed
            - jnp.mean(mixed, axis=-1, keepdims=True)
            - normed * jnp.mean(mixed * normed, axis=-1, keepdims=True)
        )
        + grad_float
    )
    grad_input = grad_input.astype(jnp.bfloat16)
    return (
        output,
        grad_input,
        gain_one,
        shift_one,
        gain_two,
        shift_two,
        grad_qkv_weight,
        grad_qkv_bias,
        grad_out_weight,
        bias_total,
        grad_up_weight,
        grad_up_bias,
        grad_down_weight,
        bias_total,
    )


def solution(mesh):
    placed = (
        P(("dp", "tensor"), None),
        P("dp", None),
        P(),
        P(),
        P(),
        P(),
        P(None, "tensor"),
        P("tensor"),
        P("tensor", None),
        P(),
        P(None, "tensor"),
        P("tensor"),
        P("tensor", None),
        P(),
        P(("dp", "tensor"), None),
    )
    return jax.shard_map(
        shards,
        mesh=mesh,
        in_specs=placed,
        out_specs=(
            P(("dp", "tensor"), None),
            P(("dp", "tensor"), None),
            P(),
            P(),
            P(),
            P(),
            P("dp", "tensor"),
            P("tensor"),
            P("tensor", "dp"),
            P(),
            P("dp", "tensor"),
            P("tensor"),
            P("tensor", "dp"),
            P(),
        ),
        check_vma=False,
    )
```

```python
import math

import jax
import jax.numpy as jnp
from jax import lax
from jax.experimental import pallas as pl
from jax.experimental.pallas import tpu as pltpu
from jax.sharding import PartitionSpec as P


HD = 64
ROT = 16


epsilon = 1e-05
masked_score = 1e30
inv_sqrt_two = 0.7071067811865476
inv_sqrt_two_pi = 0.3989422804014327


TN = ((0,), (0,))
NN = ((1,), (0,))
NT = ((1,), (1,))


def token_places(ids_ref, axis, shape):
    blocks = ids_ref.shape[0]
    size = shape[axis] // blocks
    place = lax.broadcasted_iota(jnp.int32, shape, axis)
    found = place + ids_ref[0]
    for block in range(1, blocks):
        shift = ids_ref[block] - block * size
        found = jnp.where(place >= block * size, place + shift, found)
    return found


def rotary_and_mask(ids_ref, lengths_ref, rows):
    columns = 2 * HD
    half = ROT // 2
    ids = token_places(ids_ref, 0, (rows, columns))
    first_token = jnp.zeros_like(ids)
    start = jnp.int32(0)
    for index in range(lengths_ref.shape[1]):
        first_token = jnp.where(ids >= start, start, first_token)
        start = start + lengths_ref[0, index]
    position = (ids - first_token).astype(jnp.float32)
    lane = lax.broadcasted_iota(jnp.int32, (1, columns), 1)
    within = lane % HD
    power = (within % half).astype(jnp.float32) * (-2.0 / ROT * math.log(10000.0))
    angles = position * jnp.where(within < ROT, jnp.exp(power), 0.0)
    cosine = jnp.cos(angles)
    sine = jnp.sin(angles)
    left = lane < HD

    def spread(pattern, rest):
        return jnp.concatenate(
            [pattern, jnp.where(left, rest, pattern), jnp.where(left, pattern, rest)], axis=1
        )

    direct = spread(cosine, 1.0)
    later = spread(jnp.where(within < half, -sine, 0.0), 0.0)
    earlier = spread(jnp.where(within < half, 0.0, sine), 0.0)
    keys = token_places(ids_ref, 1, (1, rows))
    allowed = (keys >= first_token[:, :1]) & (keys <= ids[:, :1])
    return direct, later, earlier, jnp.where(allowed, 0.0, -masked_score)


def pack_body(affine_ref, weight_ref, target_ref):
    del weight_ref
    target_ref[...] = affine_ref[...]


def pack(affine, weight):
    in_vmem = pl.BlockSpec(memory_space=pltpu.VMEM)
    return pl.pallas_call(
        pack_body,
        in_specs=[in_vmem] * 2,
        out_specs=in_vmem,
        out_shape=jax.ShapeDtypeStruct(affine.shape, affine.dtype),
        compiler_params=pltpu.CompilerParams(vmem_limit_bytes=4 << 20),
        name="pack",
    )(affine, weight)


def copy_relative(places_ref, start, target_ref, source_ref):
    size = 128
    count = target_ref.shape[1] // size
    for place in range(count):
        origin = pl.multiple_of(places_ref[start + place] * size, size)
        target_ref[:, place * size : (place + 1) * size] = source_ref[:, pl.ds(origin, size)]


def fetch(row_refs, target_ref, arrival):
    size = row_refs[0].shape[0]
    copies = [
        pltpu.make_async_copy(
            row_ref, target_ref.at[pl.ds(index * size, size), :], arrival.at[index]
        )
        for index, row_ref in enumerate(row_refs)
    ]
    for copy in copies:
        copy.start()
    return copies


def piece_specs(pieces):
    own = pl.BlockSpec(memory_space=pltpu.HBM)
    return [own] + [pl.BlockSpec(memory_space=pl.ANY)] * (len(pieces) - 1)


def front_body(*refs, blocks, relative):
    refs = list(refs)
    places_ref = refs.pop(0)
    row_refs = [refs.pop(0) for _ in range(blocks)]
    affine_ref, weight_ref, second_ref, active_ref, slope_ref = (refs.pop(0) for _ in range(5))
    arrival, rows_ref = refs.pop(-1), refs.pop(-1)
    size = row_refs[0].shape[0]
    for index, copy in enumerate(fetch(row_refs, rows_ref, arrival)):
        copy.wait()
        rows = slice(index * size, (index + 1) * size)
        normed, _ = normalize(rows_ref[rows, :].astype(jnp.float32))
        second_ref[rows, :] = (normed * affine_ref[2:3, :] + affine_ref[3:4, :]).astype(
            jnp.bfloat16
        )
    if relative:
        copy_relative(places_ref, second_ref.shape[1] // 128, refs[0], second_ref)
    hidden = (
        lax.dot_general(
            second_ref[...], weight_ref[...], (NN, ((), ())), preferred_element_type=jnp.float32
        )
        + jnp.concatenate(
            [affine_ref[row : row + 1, :] for row in range(4, affine_ref.shape[0])], axis=1
        )
    )
    cumulative = 0.5 * (1.0 + lax.erf(hidden * inv_sqrt_two))
    active_ref[...] = (hidden * cumulative).astype(jnp.bfloat16)
    slope_ref[...] = cumulative + hidden * jnp.exp(-0.5 * hidden * hidden) * inv_sqrt_two_pi


def front(places, pieces, affine, weight, relative):
    size, width = pieces[0].shape
    rows = size * len(pieces)
    units = weight.shape[1]
    in_smem = pl.BlockSpec(memory_space=pltpu.SMEM)
    in_vmem = pl.BlockSpec(memory_space=pltpu.VMEM)
    narrow = jax.ShapeDtypeStruct((rows, width), jnp.bfloat16)
    shapes = [
        narrow,
        jax.ShapeDtypeStruct((rows, units), jnp.bfloat16),
        jax.ShapeDtypeStruct((rows, units), jnp.float32),
    ]
    shapes += [narrow] if relative else []
    return pl.pallas_call(
        lambda *refs: front_body(*refs, blocks=len(pieces), relative=relative),
        in_specs=[in_smem] + piece_specs(pieces) + [in_vmem] * 2,
        out_specs=[in_vmem] * len(shapes),
        out_shape=shapes,
        scratch_shapes=[
            pltpu.VMEM((rows, width), jnp.bfloat16),
            pltpu.SemaphoreType.DMA((len(pieces),)),
        ],
        compiler_params=pltpu.CompilerParams(vmem_limit_bytes=14 << 20),
        name="front",
    )(places, *pieces, affine, weight)


def join_body(*refs, blocks, relative):
    refs = list(refs)
    places_ref = refs.pop(0)
    row_refs = [refs.pop(0) for _ in range(blocks)]
    arrival = refs.pop(-1)
    whole_ref = refs.pop(0)
    for copy in fetch(row_refs, whole_ref, arrival):
        copy.wait()
    if relative:
        copy_relative(places_ref, 0, refs[0], whole_ref)


def join(places, pieces, relative):
    size, width = pieces[0].shape
    rows = size * len(pieces)
    in_smem = pl.BlockSpec(memory_space=pltpu.SMEM)
    in_vmem = pl.BlockSpec(memory_space=pltpu.VMEM)
    shapes = [jax.ShapeDtypeStruct((rows, width), jnp.bfloat16)] * (2 if relative else 1)
    return pl.pallas_call(
        lambda *refs: join_body(*refs, blocks=len(pieces), relative=relative),
        in_specs=[in_smem] + piece_specs(pieces),
        out_specs=[in_vmem] * len(shapes),
        out_shape=shapes,
        scratch_shapes=[pltpu.SemaphoreType.DMA((len(pieces),))],
        compiler_params=pltpu.CompilerParams(vmem_limit_bytes=8 << 20),
        name="join",
    )(places, *pieces)


def norm_body(*refs, blocks, relative):
    refs = list(refs)
    places_ref = refs.pop(0)
    row_refs = [refs.pop(0) for _ in range(blocks)]
    affine_ref, grad_ref = (refs.pop(0) for _ in range(2))
    first_ref, normed_ref, scale_ref, sum_ref = (refs.pop(0) for _ in range(4))
    arrival, rows_ref = refs.pop(-1), refs.pop(-1)
    size = row_refs[0].shape[0]
    for index, copy in enumerate(fetch(row_refs, rows_ref, arrival)):
        copy.wait()
        rows = slice(index * size, (index + 1) * size)
        normed, inv_std = normalize(rows_ref[rows, :].astype(jnp.float32))
        normed_ref[rows, :] = normed
        first_ref[rows, :] = (normed * affine_ref[0:1, :] + affine_ref[1:2, :]).astype(jnp.bfloat16)
        if index == 0:
            scale_ref[...] = inv_std
    sum_ref[...] = jnp.sum(grad_ref[...].astype(jnp.float32), axis=0, keepdims=True)
    if relative:
        count = first_ref.shape[1] // 128
        copy_relative(places_ref, 0, refs[0], first_ref)
        copy_relative(places_ref, count, refs[1], grad_ref)


def norm(places, pieces, affine, grad_rows, relative):
    size, width = pieces[0].shape
    rows = size * len(pieces)
    in_smem = pl.BlockSpec(memory_space=pltpu.SMEM)
    in_vmem = pl.BlockSpec(memory_space=pltpu.VMEM)
    narrow = jax.ShapeDtypeStruct((rows, width), jnp.bfloat16)
    shapes = [
        narrow,
        jax.ShapeDtypeStruct((rows, width), jnp.float32),
        jax.ShapeDtypeStruct((size, 1), jnp.float32),
        jax.ShapeDtypeStruct((1, width), jnp.float32),
    ]
    shapes += [narrow] * 2 if relative else []
    return pl.pallas_call(
        lambda *refs: norm_body(*refs, blocks=len(pieces), relative=relative),
        in_specs=[in_smem] + piece_specs(pieces) + [in_vmem] * 2,
        out_specs=[in_vmem] * len(shapes),
        out_shape=shapes,
        scratch_shapes=[
            pltpu.VMEM((rows, width), jnp.bfloat16),
            pltpu.SemaphoreType.DMA((len(pieces),)),
        ],
        compiler_params=pltpu.CompilerParams(vmem_limit_bytes=8 << 20),
        name="norm",
    )(places, *pieces, affine, grad_rows)


def mix_body(
    d_joined_ref,
    qkv_ref,
    d_hidden_ref,
    up_ref,
    normed_ref,
    affine_ref,
    flat_ref,
    out_ref,
    active_ref,
    down_ref,
    keep_ref,
    send_ref,
    sums_ref,
):
    def product(left_ref, right_ref, dims):
        return lax.dot_general(
            left_ref[...], right_ref[...], (dims, ((), ())), preferred_element_type=jnp.float32
        )

    d_first = product(d_joined_ref, qkv_ref, NT)
    d_second = product(d_hidden_ref, up_ref, NT)
    normed = normed_ref[...]
    width = normed.shape[1]
    sums_ref[0:1, :] = jnp.sum(d_first * normed, axis=0, keepdims=True)
    sums_ref[1:2, :] = jnp.sum(d_first, axis=0, keepdims=True)
    sums_ref[2:3, :] = jnp.sum(d_second * normed, axis=0, keepdims=True)
    sums_ref[3:4, :] = jnp.sum(d_second, axis=0, keepdims=True)
    mixed = d_first * affine_ref[0:1, :] + d_second * affine_ref[2:3, :]
    branch = product(flat_ref, out_ref, NN) + product(active_ref, down_ref, NN)
    half = keep_ref.shape[0]
    for start, part in ((0, mixed), (width, branch)):
        columns = slice(start, start + width)
        keep_ref[:, columns] = part[:half]
        send_ref[:, columns] = part[half:].astype(jnp.bfloat16)


def mix(d_joined, qkv_weight, d_hidden, up_weight, normed, affine, flat, out_weight, active, down):
    rows, width = normed.shape
    in_vmem = pl.BlockSpec(memory_space=pltpu.VMEM)
    return pl.pallas_call(
        mix_body,
        in_specs=[in_vmem] * 10,
        out_specs=[in_vmem] * 3,
        out_shape=[
            jax.ShapeDtypeStruct((rows // 2, 2 * width), jnp.float32),
            jax.ShapeDtypeStruct((rows // 2, 2 * width), jnp.bfloat16),
            jax.ShapeDtypeStruct((4, width), jnp.float32),
        ],
        compiler_params=pltpu.CompilerParams(vmem_limit_bytes=16 << 20),
        name="mix",
    )(d_joined, qkv_weight, d_hidden, up_weight, normed, affine, flat, out_weight, active, down)


def attention_body(
    first_ref,
    weight_ref,
    bias_ref,
    grad_ref,
    out_ref,
    ids_ref,
    lengths_ref,
    flat_ref,
    d_joined_ref,
    bias_sum_ref,
    turned_ref,
    d_turned_ref,
):
    heads = weight_ref.shape[1] // (3 * HD)
    half = ROT // 2
    scale = 1.0 / math.sqrt(HD)

    def columns(head, kind):
        start = (3 * head + kind) * HD
        return slice(start, start + HD)

    joined = (
        lax.dot_general(
            first_ref[...], weight_ref[...], (NN, ((), ())), preferred_element_type=jnp.float32
        )
        + bias_ref[...]
    )
    total = joined.shape[1]

    direct, later, earlier, mask = rotary_and_mask(ids_ref, lengths_ref, joined.shape[0])
    direct, later, earlier = (
        jnp.concatenate([part] * (heads // 2), axis=1) for part in (direct, later, earlier)
    )
    turned_ref[...] = (
        joined * direct
        + pltpu.roll(joined, total - half, 1) * later
        + pltpu.roll(joined, half, 1) * earlier
    ).astype(jnp.bfloat16)
    d_attended_all = lax.dot_general(
        grad_ref[...], out_ref[...], (NT, ((), ())), preferred_element_type=jnp.float32
    ).astype(jnp.bfloat16)

    def product(left, right, dims):
        return lax.dot_general(left, right, (dims, ((), ())), preferred_element_type=jnp.float32)

    for head in range(heads):
        query = turned_ref[:, columns(head, 0)]
        key = turned_ref[:, columns(head, 1)]
        value = turned_ref[:, columns(head, 2)]
        d_attended = d_attended_all[:, head * HD : (head + 1) * HD]
        scores = product(query, key, NT) * scale + mask
        peak = jnp.max(scores, axis=1, keepdims=True)
        expo = jnp.exp(scores - peak)
        probs = expo / jnp.sum(expo, axis=1, keepdims=True)
        probs_b = probs.astype(jnp.bfloat16)
        attended = product(probs_b, value, NN).astype(jnp.bfloat16)
        flat_ref[:, head * HD : (head + 1) * HD] = attended
        d_probs = product(d_attended, value, NT)
        delta = jnp.sum(
            d_attended.astype(jnp.float32) * attended.astype(jnp.float32), axis=1, keepdims=True
        )
        d_scores = (probs * (d_probs - delta) * scale).astype(jnp.bfloat16)
        d_turned_ref[:, columns(head, 0)] = product(d_scores, key, NN)
        d_turned_ref[:, columns(head, 1)] = product(d_scores, query, TN)
        d_turned_ref[:, columns(head, 2)] = product(probs_b, d_attended, TN)
    d_turned = d_turned_ref[...]
    d_joined = (
        d_turned * direct
        - pltpu.roll(d_turned, total - half, 1) * later
        - pltpu.roll(d_turned, half, 1) * earlier
    )
    bias_sum_ref[...] = jnp.sum(d_joined, axis=0, keepdims=True)
    d_joined_ref[...] = d_joined.astype(jnp.bfloat16)


def attention(first_in, weight, bias, grad_rows, out_weight, block_ids, lengths):
    rows = first_in.shape[0]
    columns = weight.shape[1]
    in_vmem = pl.BlockSpec(memory_space=pltpu.VMEM)
    return pl.pallas_call(
        attention_body,
        in_specs=[in_vmem] * 5 + [pl.BlockSpec(memory_space=pltpu.SMEM)] * 2,
        out_specs=[in_vmem] * 3,
        out_shape=[
            jax.ShapeDtypeStruct((rows, columns // 3), jnp.bfloat16),
            jax.ShapeDtypeStruct((rows, columns), jnp.bfloat16),
            jax.ShapeDtypeStruct((1, columns), jnp.float32),
        ],
        scratch_shapes=[
            pltpu.VMEM((rows, columns), jnp.bfloat16),
            pltpu.VMEM((rows, columns), jnp.float32),
        ],
        compiler_params=pltpu.CompilerParams(vmem_limit_bytes=16 << 20),
        name="attention",
    )(
        first_in,
        weight,
        bias[None, :],
        grad_rows,
        out_weight,
        block_ids,
        lengths,
    )


def normalize(inputs):
    centered = inputs - jnp.mean(inputs, axis=-1, keepdims=True)
    inv_std = lax.rsqrt(jnp.mean(centered * centered, axis=-1, keepdims=True) + epsilon)
    return (centered * inv_std, inv_std)


def swap(array, axis, bit):
    count = lax.axis_size(axis)
    return lax.ppermute(array, axis, [(i, i ^ (1 << bit)) for i in range(count)])


def axis_bits(axis):
    return lax.axis_size(axis).bit_length() - 1


def relatives(bits):
    found = [0]
    for bit in reversed(bits):
        found = found + [relative | (1 << bit) for relative in found]
    return found


def relative_blocks(array, axis, bits, dim):
    own = lax.axis_index(axis)
    size = array.shape[dim] // lax.axis_size(axis)
    pieces = [
        lax.dynamic_slice_in_dim(array, (own ^ relative) * size, size, dim)
        for relative in relatives(bits)
    ]
    return jnp.concatenate(pieces, axis=dim)


def fold(piece, axis, bits, dim):
    count = 1 << len(bits)
    send = piece(count // 2, count).astype(jnp.bfloat16)
    arrived = []
    for depth, bit in enumerate(bits):
        arrived.append((swap(send, axis, bit), count >> (depth + 1)))
        stop = count >> (depth + 1)
        last = depth + 1 == len(bits)
        total = piece(stop // 2, stop)
        for part, held in arrived[: -1 if last else None]:
            total = total + cut(part, dim, held, stop // 2, stop)
        send = total.astype(jnp.bfloat16)
    return lax.optimization_barrier(total) + arrived[-1][0]


def cut(array, dim, count, start, stop):
    size = array.shape[dim] // count
    return lax.slice_in_dim(array, start * size, stop * size, axis=dim)


def all_sum(array, axis, bits):
    for bit in bits:
        array = array + swap(array, axis, bit)
    return array


def dot(left, right, dims):
    return lax.dot_general(left, right, (dims, ((), ())), preferred_element_type=jnp.float32)


def shards(
    tokens,
    seq_lengths,
    ln1_gain,
    ln1_bias,
    ln2_gain,
    ln2_bias,
    qkv_weight,
    qkv_bias,
    out_weight,
    out_bias,
    up_weight,
    up_bias,
    down_weight,
    down_bias,
    cotangent,
):
    row_count = tokens.shape[0]
    width = tokens.shape[1]
    tensor_bits = list(range(axis_bits("tensor")))
    dp_bits = list(range(axis_bits("dp")))
    y_first = dp_bits
    z_first = dp_bits[1:2] + dp_bits[0:1] + dp_bits[2:]
    own_rank = lax.axis_index("tensor")
    block_ids = (own_rank ^ jnp.array(relatives(tensor_bits), jnp.int32)) * row_count

    def gather(rows):
        pieces = [rows]
        for bit in reversed(tensor_bits):
            arrived = []
            for piece in pieces:
                arrived.append(swap(piece, "tensor", bit))
            pieces = pieces + arrived
        return pieces

    token_pieces = gather(tokens)
    grad_pieces = gather(cotangent)
    own_group = lax.axis_index("dp")
    places = own_group ^ jnp.array(relatives(y_first) + relatives(z_first), jnp.int32)
    affine = jnp.stack(
        [ln1_gain, ln1_bias, ln2_gain, ln2_bias, *up_bias.reshape(-1, width)]
    )
    affine = pack(affine, up_weight)
    groups = lax.axis_size("dp")
    relative = width // groups == 128
    second_in, active, slope, *second_rel = front(places, token_pieces, affine, up_weight, relative)
    grad_rows_all, *grad_y = join(places, grad_pieces, relative)
    first_in, whole_normed, inv_std, bias_total, *rest = norm(
        places, token_pieces, affine, grad_rows_all, relative
    )
    bias_total = bias_total[0]
    normed = whole_normed[:row_count]
    if relative:
        (grad_y,) = grad_y
        (second_rel,) = second_rel
        first_rel, grad_z = rest
    else:
        grad_y = relative_blocks(grad_rows_all, "dp", y_first, 1)
        first_rel = relative_blocks(first_in, "dp", y_first, 1)
        second_rel = relative_blocks(second_in, "dp", z_first, 1)
        grad_z = relative_blocks(grad_rows_all, "dp", z_first, 1)

    def by_columns(left, right):
        return lambda start, stop: dot(left, cut(right, 1, groups, start, stop), TN)

    def by_rows(left, right):
        return lambda start, stop: dot(cut(left, 1, groups, start, stop), right, TN)

    grad_down_weight = fold(by_columns(active, grad_y), "dp", y_first, 1)
    d_hidden = dot(grad_rows_all, down_weight, NT) * slope
    d_hidden_b = d_hidden.astype(jnp.bfloat16)
    g_up_bias = jnp.sum(d_hidden, axis=0)
    grad_up_weight = fold(by_rows(second_rel, d_hidden_b), "dp", z_first, 0)

    flat, d_joined_b, g_qkv_bias = attention(
        first_in,
        qkv_weight,
        qkv_bias,
        grad_rows_all,
        out_weight,
        block_ids,
        seq_lengths,
    )
    g_qkv_bias = g_qkv_bias[0]
    grad_qkv_weight = fold(by_rows(first_rel, d_joined_b), "dp", y_first, 0)
    grad_out_weight = fold(by_columns(flat, grad_z), "dp", z_first, 1)

    members = lax.axis_size("tensor")
    keep, send, norm_sums = mix(
        d_joined_b,
        qkv_weight,
        d_hidden_b,
        up_weight,
        whole_normed,
        affine,
        flat,
        out_weight,
        active,
        down_weight,
    )

    def token_piece(start, stop):
        if stop == members:
            return send
        return cut(keep, 0, members // 2, start, stop)

    both = fold(token_piece, "tensor", tensor_bits, 0)
    mixed = both[:, :width]
    branch = both[:, width:]
    norm_sums = all_sum(norm_sums.reshape(-1), "tensor", tensor_bits)
    sums = all_sum(
        jnp.concatenate([norm_sums, bias_total, g_up_bias, g_qkv_bias]),
        "dp",
        dp_bits[:1] + dp_bits[:0:-1],
    )
    gain_one, shift_one, gain_two, shift_two, bias_total = (
        sums[i * width : (i + 1) * width] for i in range(5)
    )
    rest = sums[5 * width :]
    grad_up_bias = rest[: g_up_bias.shape[0]]
    grad_qkv_bias = rest[g_up_bias.shape[0] :]

    rows_float = tokens.astype(jnp.float32)
    output = (rows_float + branch + out_bias + down_bias).astype(jnp.bfloat16)
    grad_float = cotangent.astype(jnp.float32)
    grad_input = (
        inv_std
        * (
            mixed
            - jnp.mean(mixed, axis=-1, keepdims=True)
            - normed * jnp.mean(mixed * normed, axis=-1, keepdims=True)
        )
        + grad_float
    )
    grad_input = grad_input.astype(jnp.bfloat16)
    return (
        output,
        grad_input,
        gain_one,
        shift_one,
        gain_two,
        shift_two,
        grad_qkv_weight,
        grad_qkv_bias,
        grad_out_weight,
        bias_total,
        grad_up_weight,
        grad_up_bias,
        grad_down_weight,
        bias_total,
    )


def solution(mesh):
    placed = (
        P(("dp", "tensor"), None),
        P("dp", None),
        P(),
        P(),
        P(),
        P(),
        P(None, "tensor"),
        P("tensor"),
        P("tensor", None),
        P(),
        P(None, "tensor"),
        P("tensor"),
        P("tensor", None),
        P(),
        P(("dp", "tensor"), None),
    )
    return jax.shard_map(
        shards,
        mesh=mesh,
        in_specs=placed,
        out_specs=(
            P(("dp", "tensor"), None),
            P(("dp", "tensor"), None),
            P(),
            P(),
            P(),
            P(),
            P("dp", "tensor"),
            P("tensor"),
            P("tensor", "dp"),
            P(),
            P("dp", "tensor"),
            P("tensor"),
            P("tensor", "dp"),
            P(),
        ),
        check_vma=False,
    )
```

```python
import math

import jax
import jax.numpy as jnp
from jax import lax
from jax.experimental import pallas as pl
from jax.experimental.pallas import tpu as pltpu
from jax.sharding import PartitionSpec as P


HD = 64
ROT = 16


epsilon = 1e-05
masked_score = 1e30
inv_sqrt_two = 0.7071067811865476
inv_sqrt_two_pi = 0.3989422804014327


TN = ((0,), (0,))
NN = ((1,), (0,))
NT = ((1,), (1,))


def token_places(ids_ref, axis, shape):
    blocks = ids_ref.shape[0]
    size = shape[axis] // blocks
    place = lax.broadcasted_iota(jnp.int32, shape, axis)
    found = place + ids_ref[0]
    for block in range(1, blocks):
        shift = ids_ref[block] - block * size
        found = jnp.where(place >= block * size, place + shift, found)
    return found


def rotary_and_mask(ids_ref, lengths_ref, rows):
    columns = 2 * HD
    half = ROT // 2
    ids = token_places(ids_ref, 0, (rows, columns))
    first_token = jnp.zeros_like(ids)
    start = jnp.int32(0)
    for index in range(lengths_ref.shape[1]):
        first_token = jnp.where(ids >= start, start, first_token)
        start = start + lengths_ref[0, index]
    position = (ids - first_token).astype(jnp.float32)
    lane = lax.broadcasted_iota(jnp.int32, (1, columns), 1)
    within = lane % HD
    power = (within % half).astype(jnp.float32) * (-2.0 / ROT * math.log(10000.0))
    angles = position * jnp.where(within < ROT, jnp.exp(power), 0.0)
    cosine = jnp.cos(angles)
    sine = jnp.sin(angles)
    left = lane < HD

    def spread(pattern, rest):
        return jnp.concatenate(
            [pattern, jnp.where(left, rest, pattern), jnp.where(left, pattern, rest)], axis=1
        )

    direct = spread(cosine, 1.0)
    later = spread(jnp.where(within < half, -sine, 0.0), 0.0)
    earlier = spread(jnp.where(within < half, 0.0, sine), 0.0)
    keys = token_places(ids_ref, 1, (1, rows))
    allowed = (keys >= first_token[:, :1]) & (keys <= ids[:, :1])
    return direct, later, earlier, jnp.where(allowed, 0.0, -masked_score)


def pack_body(affine_ref, weight_ref, target_ref):
    del weight_ref
    target_ref[...] = affine_ref[...]


def pack(affine, weight):
    in_vmem = pl.BlockSpec(memory_space=pltpu.VMEM)
    return pl.pallas_call(
        pack_body,
        in_specs=[in_vmem] * 2,
        out_specs=in_vmem,
        out_shape=jax.ShapeDtypeStruct(affine.shape, affine.dtype),
        compiler_params=pltpu.CompilerParams(vmem_limit_bytes=4 << 20),
        name="pack",
    )(affine, weight)


def copy_relative(places_ref, start, target_ref, source_ref):
    size = 128
    count = target_ref.shape[1] // size
    for place in range(count):
        origin = pl.multiple_of(places_ref[start + place] * size, size)
        target_ref[:, place * size : (place + 1) * size] = source_ref[:, pl.ds(origin, size)]


def fetch(row_refs, target_ref, arrival):
    size = row_refs[0].shape[0]
    copies = [
        pltpu.make_async_copy(
            row_ref, target_ref.at[pl.ds(index * size, size), :], arrival.at[index]
        )
        for index, row_ref in enumerate(row_refs)
    ]
    for copy in copies:
        copy.start()
    return copies


def piece_specs(pieces):
    own = pl.BlockSpec(memory_space=pltpu.HBM)
    return [own] + [pl.BlockSpec(memory_space=pl.ANY)] * (len(pieces) - 1)


def front_body(*refs, blocks, relative):
    refs = list(refs)
    places_ref = refs.pop(0)
    row_refs = [refs.pop(0) for _ in range(blocks)]
    affine_ref, weight_ref, active_ref, slope_ref, result_ref = (refs.pop(0) for _ in range(5))
    arrival, rows_ref = refs.pop(-1), refs.pop(-1)
    second_ref = refs.pop(0) if relative else result_ref
    size = row_refs[0].shape[0]
    for index, copy in enumerate(fetch(row_refs, rows_ref, arrival)):
        copy.wait()
        rows = slice(index * size, (index + 1) * size)
        normed, _ = normalize(rows_ref[rows, :].astype(jnp.float32))
        second_ref[rows, :] = (normed * affine_ref[2:3, :] + affine_ref[3:4, :]).astype(
            jnp.bfloat16
        )
    if relative:
        copy_relative(places_ref, second_ref.shape[1] // 128, result_ref, second_ref)
    hidden = (
        lax.dot_general(
            second_ref[...], weight_ref[...], (NN, ((), ())), preferred_element_type=jnp.float32
        )
        + jnp.concatenate(
            [affine_ref[row : row + 1, :] for row in range(4, affine_ref.shape[0])], axis=1
        )
    )
    cumulative = 0.5 * (1.0 + lax.erf(hidden * inv_sqrt_two))
    active_ref[...] = (hidden * cumulative).astype(jnp.bfloat16)
    slope_ref[...] = cumulative + hidden * jnp.exp(-0.5 * hidden * hidden) * inv_sqrt_two_pi


def front(places, pieces, affine, weight, relative):
    size, width = pieces[0].shape
    rows = size * len(pieces)
    units = weight.shape[1]
    in_smem = pl.BlockSpec(memory_space=pltpu.SMEM)
    in_vmem = pl.BlockSpec(memory_space=pltpu.VMEM)
    narrow = jax.ShapeDtypeStruct((rows, width), jnp.bfloat16)
    shapes = [
        jax.ShapeDtypeStruct((rows, units), jnp.bfloat16),
        jax.ShapeDtypeStruct((rows, units), jnp.float32),
        narrow,
    ]
    scratch = pltpu.VMEM((rows, width), jnp.bfloat16)
    return pl.pallas_call(
        lambda *refs: front_body(*refs, blocks=len(pieces), relative=relative),
        in_specs=[in_smem] + piece_specs(pieces) + [in_vmem] * 2,
        out_specs=[in_vmem] * len(shapes),
        out_shape=shapes,
        scratch_shapes=[scratch] * (2 if relative else 1)
        + [pltpu.SemaphoreType.DMA((len(pieces),))],
        compiler_params=pltpu.CompilerParams(vmem_limit_bytes=14 << 20),
        name="front",
    )(places, *pieces, affine, weight)


def join_body(*refs, blocks, relative):
    refs = list(refs)
    places_ref = refs.pop(0)
    row_refs = [refs.pop(0) for _ in range(blocks)]
    arrival = refs.pop(-1)
    whole_ref = refs.pop(0)
    for copy in fetch(row_refs, whole_ref, arrival):
        copy.wait()
    if relative:
        copy_relative(places_ref, 0, refs[0], whole_ref)


def join(places, pieces, relative):
    size, width = pieces[0].shape
    rows = size * len(pieces)
    in_smem = pl.BlockSpec(memory_space=pltpu.SMEM)
    in_vmem = pl.BlockSpec(memory_space=pltpu.VMEM)
    shapes = [jax.ShapeDtypeStruct((rows, width), jnp.bfloat16)] * (2 if relative else 1)
    return pl.pallas_call(
        lambda *refs: join_body(*refs, blocks=len(pieces), relative=relative),
        in_specs=[in_smem] + piece_specs(pieces),
        out_specs=[in_vmem] * len(shapes),
        out_shape=shapes,
        scratch_shapes=[pltpu.SemaphoreType.DMA((len(pieces),))],
        compiler_params=pltpu.CompilerParams(vmem_limit_bytes=8 << 20),
        name="join",
    )(places, *pieces)


def norm_body(*refs, blocks, relative):
    refs = list(refs)
    places_ref = refs.pop(0)
    row_refs = [refs.pop(0) for _ in range(blocks)]
    affine_ref, grad_ref = (refs.pop(0) for _ in range(2))
    first_ref, normed_ref, scale_ref, sum_ref = (refs.pop(0) for _ in range(4))
    arrival, rows_ref = refs.pop(-1), refs.pop(-1)
    size = row_refs[0].shape[0]
    for index, copy in enumerate(fetch(row_refs, rows_ref, arrival)):
        copy.wait()
        rows = slice(index * size, (index + 1) * size)
        normed, inv_std = normalize(rows_ref[rows, :].astype(jnp.float32))
        normed_ref[rows, :] = normed
        first_ref[rows, :] = (normed * affine_ref[0:1, :] + affine_ref[1:2, :]).astype(jnp.bfloat16)
        if index == 0:
            scale_ref[...] = inv_std
    sum_ref[...] = jnp.sum(grad_ref[...].astype(jnp.float32), axis=0, keepdims=True)
    if relative:
        count = first_ref.shape[1] // 128
        copy_relative(places_ref, 0, refs[0], first_ref)
        copy_relative(places_ref, count, refs[1], grad_ref)


def norm(places, pieces, affine, grad_rows, relative):
    size, width = pieces[0].shape
    rows = size * len(pieces)
    in_smem = pl.BlockSpec(memory_space=pltpu.SMEM)
    in_vmem = pl.BlockSpec(memory_space=pltpu.VMEM)
    narrow = jax.ShapeDtypeStruct((rows, width), jnp.bfloat16)
    shapes = [
        narrow,
        jax.ShapeDtypeStruct((rows, width), jnp.float32),
        jax.ShapeDtypeStruct((size, 1), jnp.float32),
        jax.ShapeDtypeStruct((1, width), jnp.float32),
    ]
    shapes += [narrow] * 2 if relative else []
    return pl.pallas_call(
        lambda *refs: norm_body(*refs, blocks=len(pieces), relative=relative),
        in_specs=[in_smem] + piece_specs(pieces) + [in_vmem] * 2,
        out_specs=[in_vmem] * len(shapes),
        out_shape=shapes,
        scratch_shapes=[
            pltpu.VMEM((rows, width), jnp.bfloat16),
            pltpu.SemaphoreType.DMA((len(pieces),)),
        ],
        compiler_params=pltpu.CompilerParams(vmem_limit_bytes=8 << 20),
        name="norm",
    )(places, *pieces, affine, grad_rows)


def mix_body(
    d_joined_ref,
    qkv_ref,
    d_hidden_ref,
    up_ref,
    normed_ref,
    affine_ref,
    flat_ref,
    out_ref,
    active_ref,
    down_ref,
    keep_ref,
    send_ref,
    sums_ref,
):
    def product(left_ref, right_ref, dims):
        return lax.dot_general(
            left_ref[...], right_ref[...], (dims, ((), ())), preferred_element_type=jnp.float32
        )

    d_first = product(d_joined_ref, qkv_ref, NT)
    d_second = product(d_hidden_ref, up_ref, NT)
    normed = normed_ref[...]
    width = normed.shape[1]
    sums_ref[0:1, :] = jnp.sum(d_first * normed, axis=0, keepdims=True)
    sums_ref[1:2, :] = jnp.sum(d_first, axis=0, keepdims=True)
    sums_ref[2:3, :] = jnp.sum(d_second * normed, axis=0, keepdims=True)
    sums_ref[3:4, :] = jnp.sum(d_second, axis=0, keepdims=True)
    mixed = d_first * affine_ref[0:1, :] + d_second * affine_ref[2:3, :]
    branch = product(flat_ref, out_ref, NN) + product(active_ref, down_ref, NN)
    half = keep_ref.shape[0]
    for start, part in ((0, mixed), (width, branch)):
        columns = slice(start, start + width)
        keep_ref[:, columns] = part[:half]
        send_ref[:, columns] = part[half:].astype(jnp.bfloat16)


def mix(d_joined, qkv_weight, d_hidden, up_weight, normed, affine, flat, out_weight, active, down):
    rows, width = normed.shape
    in_vmem = pl.BlockSpec(memory_space=pltpu.VMEM)
    return pl.pallas_call(
        mix_body,
        in_specs=[in_vmem] * 10,
        out_specs=[in_vmem] * 3,
        out_shape=[
            jax.ShapeDtypeStruct((rows // 2, 2 * width), jnp.float32),
            jax.ShapeDtypeStruct((rows // 2, 2 * width), jnp.bfloat16),
            jax.ShapeDtypeStruct((4, width), jnp.float32),
        ],
        compiler_params=pltpu.CompilerParams(vmem_limit_bytes=16 << 20),
        name="mix",
    )(d_joined, qkv_weight, d_hidden, up_weight, normed, affine, flat, out_weight, active, down)


def attention_body(
    first_ref,
    weight_ref,
    bias_ref,
    grad_ref,
    out_ref,
    ids_ref,
    lengths_ref,
    flat_ref,
    d_joined_ref,
    bias_sum_ref,
    turned_ref,
    d_turned_ref,
):
    heads = weight_ref.shape[1] // (3 * HD)
    half = ROT // 2
    scale = 1.0 / math.sqrt(HD)

    def columns(head, kind):
        start = (3 * head + kind) * HD
        return slice(start, start + HD)

    joined = (
        lax.dot_general(
            first_ref[...], weight_ref[...], (NN, ((), ())), preferred_element_type=jnp.float32
        )
        + bias_ref[...]
    )
    total = joined.shape[1]

    direct, later, earlier, mask = rotary_and_mask(ids_ref, lengths_ref, joined.shape[0])
    direct, later, earlier = (
        jnp.concatenate([part] * (heads // 2), axis=1) for part in (direct, later, earlier)
    )
    turned_ref[...] = (
        joined * direct
        + pltpu.roll(joined, total - half, 1) * later
        + pltpu.roll(joined, half, 1) * earlier
    ).astype(jnp.bfloat16)
    d_attended_all = lax.dot_general(
        grad_ref[...], out_ref[...], (NT, ((), ())), preferred_element_type=jnp.float32
    ).astype(jnp.bfloat16)

    def product(left, right, dims):
        return lax.dot_general(left, right, (dims, ((), ())), preferred_element_type=jnp.float32)

    for head in range(heads):
        query = turned_ref[:, columns(head, 0)]
        key = turned_ref[:, columns(head, 1)]
        value = turned_ref[:, columns(head, 2)]
        d_attended = d_attended_all[:, head * HD : (head + 1) * HD]
        scores = product(query, key, NT) * scale + mask
        peak = jnp.max(scores, axis=1, keepdims=True)
        expo = jnp.exp(scores - peak)
        probs = expo / jnp.sum(expo, axis=1, keepdims=True)
        probs_b = probs.astype(jnp.bfloat16)
        attended = product(probs_b, value, NN).astype(jnp.bfloat16)
        flat_ref[:, head * HD : (head + 1) * HD] = attended
        d_probs = product(d_attended, value, NT)
        delta = jnp.sum(
            d_attended.astype(jnp.float32) * attended.astype(jnp.float32), axis=1, keepdims=True
        )
        d_scores = (probs * (d_probs - delta) * scale).astype(jnp.bfloat16)
        d_turned_ref[:, columns(head, 0)] = product(d_scores, key, NN)
        d_turned_ref[:, columns(head, 1)] = product(d_scores, query, TN)
        d_turned_ref[:, columns(head, 2)] = product(probs_b, d_attended, TN)
    d_turned = d_turned_ref[...]
    d_joined = (
        d_turned * direct
        - pltpu.roll(d_turned, total - half, 1) * later
        - pltpu.roll(d_turned, half, 1) * earlier
    )
    bias_sum_ref[...] = jnp.sum(d_joined, axis=0, keepdims=True)
    d_joined_ref[...] = d_joined.astype(jnp.bfloat16)


def attention(first_in, weight, bias, grad_rows, out_weight, block_ids, lengths):
    rows = first_in.shape[0]
    columns = weight.shape[1]
    in_vmem = pl.BlockSpec(memory_space=pltpu.VMEM)
    return pl.pallas_call(
        attention_body,
        in_specs=[in_vmem] * 5 + [pl.BlockSpec(memory_space=pltpu.SMEM)] * 2,
        out_specs=[in_vmem] * 3,
        out_shape=[
            jax.ShapeDtypeStruct((rows, columns // 3), jnp.bfloat16),
            jax.ShapeDtypeStruct((rows, columns), jnp.bfloat16),
            jax.ShapeDtypeStruct((1, columns), jnp.float32),
        ],
        scratch_shapes=[
            pltpu.VMEM((rows, columns), jnp.bfloat16),
            pltpu.VMEM((rows, columns), jnp.float32),
        ],
        compiler_params=pltpu.CompilerParams(vmem_limit_bytes=16 << 20),
        name="attention",
    )(
        first_in,
        weight,
        bias[None, :],
        grad_rows,
        out_weight,
        block_ids,
        lengths,
    )


def normalize(inputs):
    centered = inputs - jnp.mean(inputs, axis=-1, keepdims=True)
    inv_std = lax.rsqrt(jnp.mean(centered * centered, axis=-1, keepdims=True) + epsilon)
    return (centered * inv_std, inv_std)


def swap(array, axis, bit):
    count = lax.axis_size(axis)
    return lax.ppermute(array, axis, [(i, i ^ (1 << bit)) for i in range(count)])


def axis_bits(axis):
    return lax.axis_size(axis).bit_length() - 1


def relatives(bits):
    found = [0]
    for bit in reversed(bits):
        found = found + [relative | (1 << bit) for relative in found]
    return found


def relative_blocks(array, axis, bits, dim):
    own = lax.axis_index(axis)
    size = array.shape[dim] // lax.axis_size(axis)
    pieces = [
        lax.dynamic_slice_in_dim(array, (own ^ relative) * size, size, dim)
        for relative in relatives(bits)
    ]
    return jnp.concatenate(pieces, axis=dim)


def fold(piece, axis, bits, dim):
    count = 1 << len(bits)
    send = piece(count // 2, count).astype(jnp.bfloat16)
    arrived = []
    for depth, bit in enumerate(bits):
        arrived.append((swap(send, axis, bit), count >> (depth + 1)))
        stop = count >> (depth + 1)
        last = depth + 1 == len(bits)
        total = piece(stop // 2, stop)
        for part, held in arrived[: -1 if last else None]:
            total = total + cut(part, dim, held, stop // 2, stop)
        send = total.astype(jnp.bfloat16)
    return lax.optimization_barrier(total) + arrived[-1][0]


def cut(array, dim, count, start, stop):
    size = array.shape[dim] // count
    return lax.slice_in_dim(array, start * size, stop * size, axis=dim)


def all_sum(array, axis, bits):
    for bit in bits:
        array = array + swap(array, axis, bit)
    return array


def dot(left, right, dims):
    return lax.dot_general(left, right, (dims, ((), ())), preferred_element_type=jnp.float32)


def shards(
    tokens,
    seq_lengths,
    ln1_gain,
    ln1_bias,
    ln2_gain,
    ln2_bias,
    qkv_weight,
    qkv_bias,
    out_weight,
    out_bias,
    up_weight,
    up_bias,
    down_weight,
    down_bias,
    cotangent,
):
    row_count = tokens.shape[0]
    width = tokens.shape[1]
    tensor_bits = list(range(axis_bits("tensor")))
    dp_bits = list(range(axis_bits("dp")))
    y_first = dp_bits
    z_first = dp_bits[1:2] + dp_bits[0:1] + dp_bits[2:]
    own_rank = lax.axis_index("tensor")
    block_ids = (own_rank ^ jnp.array(relatives(tensor_bits), jnp.int32)) * row_count

    def gather(rows):
        pieces = [rows]
        for bit in reversed(tensor_bits):
            arrived = []
            for piece in pieces:
                arrived.append(swap(piece, "tensor", bit))
            pieces = pieces + arrived
        return pieces

    token_pieces = gather(tokens)
    grad_pieces = gather(cotangent)
    own_group = lax.axis_index("dp")
    places = own_group ^ jnp.array(relatives(y_first) + relatives(z_first), jnp.int32)
    affine = jnp.stack(
        [ln1_gain, ln1_bias, ln2_gain, ln2_bias, *up_bias.reshape(-1, width)]
    )
    affine = pack(affine, up_weight)
    groups = lax.axis_size("dp")
    relative = width // groups == 128
    active, slope, second_rel = front(
        places, token_pieces, affine, up_weight, relative
    )
    grad_rows_all, *grad_y = join(places, grad_pieces, relative)
    first_in, whole_normed, inv_std, bias_total, *rest = norm(
        places, token_pieces, affine, grad_rows_all, relative
    )
    bias_total = bias_total[0]
    normed = whole_normed[:row_count]
    if relative:
        (grad_y,) = grad_y
        first_rel, grad_z = rest
    else:
        grad_y = relative_blocks(grad_rows_all, "dp", y_first, 1)
        first_rel = relative_blocks(first_in, "dp", y_first, 1)
        second_rel = relative_blocks(second_rel, "dp", z_first, 1)
        grad_z = relative_blocks(grad_rows_all, "dp", z_first, 1)

    def by_columns(left, right):
        return lambda start, stop: dot(left, cut(right, 1, groups, start, stop), TN)

    def by_rows(left, right):
        return lambda start, stop: dot(cut(left, 1, groups, start, stop), right, TN)

    grad_down_weight = fold(by_columns(active, grad_y), "dp", y_first, 1)
    d_hidden = dot(grad_rows_all, down_weight, NT) * slope
    d_hidden_b = d_hidden.astype(jnp.bfloat16)
    g_up_bias = jnp.sum(d_hidden, axis=0)
    grad_up_weight = fold(by_rows(second_rel, d_hidden_b), "dp", z_first, 0)

    flat, d_joined_b, g_qkv_bias = attention(
        first_in,
        qkv_weight,
        qkv_bias,
        grad_rows_all,
        out_weight,
        block_ids,
        seq_lengths,
    )
    g_qkv_bias = g_qkv_bias[0]
    grad_qkv_weight = fold(by_rows(first_rel, d_joined_b), "dp", y_first, 0)
    grad_out_weight = fold(by_columns(flat, grad_z), "dp", z_first, 1)

    members = lax.axis_size("tensor")
    keep, send, norm_sums = mix(
        d_joined_b,
        qkv_weight,
        d_hidden_b,
        up_weight,
        whole_normed,
        affine,
        flat,
        out_weight,
        active,
        down_weight,
    )

    def token_piece(start, stop):
        if stop == members:
            return send
        return cut(keep, 0, members // 2, start, stop)

    both = fold(token_piece, "tensor", tensor_bits, 0)
    mixed = both[:, :width]
    branch = both[:, width:]
    norm_sums = all_sum(norm_sums.reshape(-1), "tensor", tensor_bits)
    sums = all_sum(
        jnp.concatenate([norm_sums, bias_total, g_up_bias, g_qkv_bias]),
        "dp",
        dp_bits[:1] + dp_bits[:0:-1],
    )
    gain_one, shift_one, gain_two, shift_two, bias_total = (
        sums[i * width : (i + 1) * width] for i in range(5)
    )
    rest = sums[5 * width :]
    grad_up_bias = rest[: g_up_bias.shape[0]]
    grad_qkv_bias = rest[g_up_bias.shape[0] :]

    rows_float = tokens.astype(jnp.float32)
    output = (rows_float + branch + out_bias + down_bias).astype(jnp.bfloat16)
    grad_float = cotangent.astype(jnp.float32)
    grad_input = (
        inv_std
        * (
            mixed
            - jnp.mean(mixed, axis=-1, keepdims=True)
            - normed * jnp.mean(mixed * normed, axis=-1, keepdims=True)
        )
        + grad_float
    )
    grad_input = grad_input.astype(jnp.bfloat16)
    return (
        output,
        grad_input,
        gain_one,
        shift_one,
        gain_two,
        shift_two,
        grad_qkv_weight,
        grad_qkv_bias,
        grad_out_weight,
        bias_total,
        grad_up_weight,
        grad_up_bias,
        grad_down_weight,
        bias_total,
    )


def solution(mesh):
    placed = (
        P(("dp", "tensor"), None),
        P("dp", None),
        P(),
        P(),
        P(),
        P(),
        P(None, "tensor"),
        P("tensor"),
        P("tensor", None),
        P(),
        P(None, "tensor"),
        P("tensor"),
        P("tensor", None),
        P(),
        P(("dp", "tensor"), None),
    )
    return jax.shard_map(
        shards,
        mesh=mesh,
        in_specs=placed,
        out_specs=(
            P(("dp", "tensor"), None),
            P(("dp", "tensor"), None),
            P(),
            P(),
            P(),
            P(),
            P("dp", "tensor"),
            P("tensor"),
            P("tensor", "dp"),
            P(),
            P("dp", "tensor"),
            P("tensor"),
            P("tensor", "dp"),
            P(),
        ),
        check_vma=False,
    )
```
